256 devices in a mesh: row: 8 (over y, z_lo), col: 32 (over z_hi, x, core).
Axes of the slice: x: 4, y: 4, z: 8 (z_hi: 4, z_lo: 2; z = z_hi * 2 + z_lo), core: 2. Of those that a mesh axis runs over, the one named last changes fastest.
Arguments:
- grad_output: bfloat16 [1024, 8192], P('col', 'row'), may hold values from -6 to 6
- inputs: bfloat16 [1024, 28672], P('row', 'col'), may hold values from -0.1875 to 0.1875
- weight: bfloat16 [28672, 8192], P('col', 'row'), may hold values from -0.125 to 0.125
- block_mask: int32 [224, 64], P('col'), may hold values from 0 to 1, as said below
Outputs:
- grad_input: bfloat16 [1024, 28672], P('row', 'col')
- grad_weight: bfloat16 [28672, 8192], P('col', 'row')
The draws below stay inside these ranges and needn't reach their ends.
Inputs may be any that keep to these rules, and one draw needn't show every extreme that they name: `block_mask`: 1 where the 128 x 128 block of weight is kept, 0 where it is zero; the share of kept blocks differs widely from block row to block row.
All inputs are finite; a program needn't handle non-finite values.
Results may differ from the reference program's by a relative error of at most 0.001.
Values may be sent and summed in bfloat16 or wider, within the bound.
A program may use at most 64 MiB of HBM per device.

```python
import jax
import jax.numpy as jnp
from jax import lax

D = 8192
H = 28672
BLOCK = 128
TOKENS = 1024
HB = 224
DB = 64


def draw_block_mask(key, part):
    level_key, cell_key = jax.random.split(jax.random.fold_in(key, 7))
    levels = jax.random.randint(level_key, (HB, 1), 0, 4)
    percent = jnp.array([8, 18, 36, 58], jnp.int32)[levels]
    rolls = jax.random.randint(cell_key, (HB, DB), 0, 100)
    return (rolls < percent).astype(jnp.int32)


def block_levels(rng, shape, shards, smallest, top_value):
    def one(dim, shards_of):
        draws = jax.random.uniform(jax.random.fold_in(jax.random.fold_in(rng, 6), dim), (shards_of,), jnp.float32, smallest / len(shards), top_value / len(shards))
        return jnp.repeat(jnp.exp(draws), shape[dim] // shards_of).reshape((-1,) + (1,) * (len(shape) - dim - 1))

    factor_of = one(*shards[0])
    for cut in shards[1:]:
        factor_of = factor_of * one(*cut)
    return factor_of


def centred(key, dims, width, limit, pieces=(), kind=jnp.bfloat16):
    values = width * jax.random.normal(key, dims, jnp.float32)
    if pieces:
        values = values * block_levels(key, dims, pieces, -0.22, 0.18)
    return jnp.clip(values, -limit, limit).astype(kind)


def setup_inputs(seed: int = 0) -> dict:
    splits = jax.random.split(jax.random.key(seed), 5)
    return {
        "grad_output": centred(splits[0], (TOKENS, D), 1.0, 6.0, ((0, 32), (1, 8))),
        "inputs": centred(splits[1], (TOKENS, H), (TOKENS ** -0.5), 0.1875, ((0, 8), (1, 32))),
        "weight": centred(splits[2], (H, D), (D * 3 // 10) ** -0.5, 0.125, ((0, 32), (1, 8))),
        "block_mask": draw_block_mask(jax.random.fold_in(splits[4], 71), 0),
    }


def reference(grad_output, inputs, weight, block_mask):
    mask_values = block_mask.astype(jnp.bfloat16)
    kept = (weight.reshape(HB, BLOCK, DB, BLOCK) * mask_values[:, None, :, None]).reshape(H, D)
    grad_input = jnp.dot(grad_output, kept.T, preferred_element_type=jnp.float32).astype(jnp.bfloat16)

    def one_row(row_index):
        columns = lax.dynamic_slice_in_dim(inputs, row_index * BLOCK, BLOCK, 1)
        product = lax.dot_general(columns, grad_output, (((0,), (0,)), ((), ())), preferred_element_type=jnp.float32)
        mask_row = lax.dynamic_index_in_dim(block_mask, row_index, 0, keepdims=False).astype(jnp.float32)
        masked = product.reshape(BLOCK, DB, BLOCK) * mask_row[None, :, None]
        return masked.reshape(BLOCK, D).astype(jnp.bfloat16)

    grad_weight = lax.map(one_row, jnp.arange(HB, dtype=jnp.int32)).reshape(H, D)
    return grad_input, grad_weight
```

```python
import functools

import jax
import jax.numpy as jnp
from jax import lax
from jax.experimental import pallas as pl
from jax.experimental.pallas import tpu as pltpu
from jax.sharding import PartitionSpec as P

MESH = pl.DeviceIdType.MESH
BLOCK = 128
TOKENS = 1024
MINE = 32
ROWS = 128
ZFIRST = 64
PIECE = 32
TOP = 32767.0
RELAYED = (0, 1, -1)


def wrap(v, n):
    return lax.rem(v + n, n)


def kernel(
    g_hbm, in_hbm, w_hbm, mask_hbm, gi_out, gw_out,
    mask, gi_ref, gw_ref, gall, inall, flipped, kept, part,
    code_out, code_in, scale_out, scale_in,
    ssem, rsem, lsem,
):
    row, col = lax.axis_index("row"), lax.axis_index("col")
    y, zl = row // 2, lax.rem(row, 2)
    zh, x, k = col // 8, lax.rem(col // 2, 4), lax.rem(col, 2)
    hid, wid = w_hbm.shape

    def dev(dy=0, flip=False, dzh=0, dx=0, core=False):
        z = 1 - zl if flip else zl
        c = 1 - k if core else k
        return (wrap(y + dy, 4) * 2 + z, (wrap(zh + dzh, 4) * 4 + wrap(x + dx, 4)) * 2 + c)

    peers = [
        dev(dy=1), dev(dy=-1), dev(flip=True), dev(dzh=1), dev(dzh=-1),
        dev(dx=1), dev(dx=-1), dev(core=True),
    ]
    peers.append(dev(dx=2))

    load_g = pltpu.make_async_copy(
        g_hbm, gall.at[pl.ds(pl.multiple_of(col * MINE, MINE), MINE)], lsem.at[0]
    )
    load_in = pltpu.make_async_copy(
        in_hbm, inall.at[pl.ds(pl.multiple_of(row * ROWS, ROWS), ROWS)], lsem.at[1]
    )
    load_w = pltpu.make_async_copy(w_hbm, kept, lsem.at[2])
    load_mask = pltpu.make_async_copy(mask_hbm, mask, lsem.at[3])
    for load in (load_g, load_in, load_mask, load_w):
        load.start()

    barrier = pltpu.get_barrier_semaphore()
    for peer in peers:
        pl.semaphore_signal(barrier, inc=1, device_id=peer, device_id_type=MESH)
    pl.semaphore_wait(barrier, len(peers))
    load_g.wait()
    load_in.wait()

    kinds = {"g": gall, "in": inall, "code": code_out, "scale": scale_out}
    order = list(kinds)
    leading = dict.fromkeys(kinds, 0)
    names = {}

    def remote(kind, name, src, dst, device):
        i = names.setdefault(name, len(names))
        return pltpu.make_async_remote_copy(
            src_ref=src, dst_ref=dst, send_sem=ssem.at[order.index(kind)], recv_sem=rsem.at[i],
            device_id=device, device_id_type=MESH,
        )

    def send(kind, name, src, dst, device):
        leading[kind] += src.shape[0]
        remote(kind, name, src, dst, device).start()

    def arrived(name, ref):
        remote("g", name, ref, ref, dev(core=True)).wait_recv()

    def g(dz, dx, half=None):
        at = ((wrap(zh + dz, 4) * 4 + wrap(x + dx, 4)) * 2 + k) * MINE
        if half is None:
            return gall.at[pl.ds(pl.multiple_of(at, MINE), MINE)]
        n = MINE // 2
        return gall.at[pl.ds(pl.multiple_of(at + half * n, n), n)]

    def send_g(name, ref, device):
        send("g", name, ref, ref, device)

    def across(d, e):
        send_g("c", g(d, e), dev(core=True))

    def spread_x(d):
        send_g(("xp", d), g(d, 0), dev(dx=1))
        send_g(("xm", d), g(d, 0), dev(dx=-1))
        if d not in RELAYED:
            send_g(("x2", d), g(d, 0), dev(dx=2))
        across(d, 0)

    def relay_x(d):
        arrived(("xp", d), g(d, -1))
        if d in RELAYED:
            send_g(("x2", d), g(d, -1, 0), dev(dx=1))
        across(d, -1)
        arrived(("xm", d), g(d, 1))
        if d in RELAYED:
            send_g(("x2", d), g(d, 1, 1), dev(dx=-1))
        across(d, 1)

    def finish_x(d):
        arrived(("x2", d), g(d, 2))
        across(d, 2)

    def rows_in(dy, flip, lo, n):
        z = 1 - zl if flip else zl
        at = (wrap(y + dy, 4) * 2 + z) * ROWS + lo
        return inall.at[pl.ds(pl.multiple_of(at, 16), n)]

    def send_in(name, dy, flip, lo, n, device):
        ref = rows_in(dy, flip, lo, n)
        send("in", name, ref, ref, device)

    def spread_y(tag, flip, lo, n):
        send_in("iyp" + tag, 0, flip, lo, n, dev(dy=1))
        send_in("iym" + tag, 0, flip, lo, n, dev(dy=-1))

    def relay_y(tag, flip, lo, n):
        h = n // 2
        arrived("iyp" + tag, rows_in(-1, flip, lo, n))
        send_in("iy2" + tag, -1, flip, lo, h, dev(dy=1))
        arrived("iym" + tag, rows_in(1, flip, lo, n))
        send_in("iy2" + tag, 1, flip, lo + h, h, dev(dy=-1))

    zn, yn = ZFIRST, ROWS - ZFIRST

    send_g("zp", g(0, 0), dev(dzh=1))
    send_g("zm", g(0, 0), dev(dzh=-1))
    spread_x(0)
    spread_y("1", False, zn, yn)
    spread_y("0", False, 0, zn)
    send_in("iz", 0, False, 0, zn, dev(flip=True))

    load_mask.wait()
    load_w.wait()

    def mask_row(i, _):
        rows = pl.ds(pl.multiple_of(i * BLOCK, BLOCK), BLOCK)
        for j in range(wid // BLOCK):
            cols = pl.ds(j * BLOCK, BLOCK)
            m = mask[i, row * (wid // BLOCK) + j].astype(jnp.float32)
            kept[rows, cols] = (kept[rows, cols].astype(jnp.float32) * m).astype(jnp.bfloat16)
        return 0

    lax.fori_loop(0, hid // BLOCK, mask_row, 0)

    relay_x(0)
    arrived("zp", g(-1, 0))
    send_g("z2", g(-1, 0, 0), dev(dzh=1))
    spread_x(-1)
    arrived("zm", g(1, 0))
    send_g("z2", g(1, 0, 1), dev(dzh=-1))
    spread_x(1)
    relay_y("1", False, zn, yn)
    finish_x(0)
    relay_y("0", False, 0, zn)
    arrived("iz", rows_in(0, True, 0, zn))
    spread_y("2", True, 0, zn)
    relay_x(-1)
    arrived("z2", g(2, 0))
    spread_x(2)
    send_in("jz", 0, False, zn, yn, dev(flip=True))
    send_in("jz", -1, False, zn, yn, dev(flip=True))
    send_in("jz", 1, False, zn, yn, dev(flip=True))
    relay_x(1)
    arrived("iy21", rows_in(2, False, zn, yn))
    send_in("jz", 2, False, zn, yn, dev(flip=True))
    finish_x(-1)
    finish_x(1)
    relay_x(2)
    relay_y("2", True, 0, zn)
    finish_x(2)
    arrived("c", gall.at[pl.ds(0, TOKENS // 2)])

    def multiply(i, dy):
        tokens = gall[pl.ds(pl.multiple_of(wrap(y + dy, 4) * 256, 256), 256), :]
        for lo in range(0, hid, 256):
            n = min(256, hid - lo)
            part[i, :, pl.ds(lo, n)] = lax.dot_general(
                tokens, kept[pl.ds(lo, n), :], (((1,), (1,)), ((), ())),
                preferred_element_type=jnp.float32,
            )

    def piece(i, q, w, late=0):
        z = zl if q else 1 - zl
        at = z * ROWS + late * 2 * PIECE + w * PIECE
        return part[i, pl.ds(pl.multiple_of(at, PIECE), PIECE), :]

    slots = {}
    used = [0, 0]

    def post(name, sem, values, device):
        c, m, n = slots[name] = (used[0], used[1], len(values))
        used[0] += n
        used[1] += 1
        top = functools.reduce(
            jnp.maximum, [jnp.max(jnp.abs(v), axis=0, keepdims=True) for v in values]
        )
        top = jnp.maximum(top, 1e-30)
        scale_out[m] = top * (1.0 / TOP)
        for j, v in enumerate(values):
            code_out[c + j] = jnp.round(v * (TOP / top)).astype(jnp.int32).astype(jnp.int16)
        cs, ms = pl.ds(c, n), pl.ds(m, 1)
        send("scale", (sem, "s"), scale_out.at[ms], scale_in.at[ms], device)
        send("code", (sem, "q"), code_out.at[cs], code_in.at[cs], device)

    def wait_for(sem, messages, n):
        arrived((sem, "s"), scale_in.at[pl.ds(0, messages)])
        arrived((sem, "q"), code_in.at[pl.ds(0, messages * n)])

    def decode(name, j=0):
        c, m, _ = slots[name]
        return code_in[c + j].astype(jnp.int32).astype(jnp.float32) * scale_in[m]

    ways = ((0, 1, 1), (1, 3, -1))

    def first(qs):
        for w, _, s in ways:
            post(("m1", qs, w), ("m1", qs), [piece(2, q, w) for q in qs], dev(dy=s))

    def second(qs, way):
        w, i, s = way
        post(("m2", qs, w), ("m2", qs), [piece(i, q, 1 - w) for q in qs], dev(dy=s))

    def third(qs):
        wait_for(("m1", qs), 2, len(qs))
        for w, i, s in ways:
            values = [piece(i, q, w) + decode(("m1", qs, w), j) for j, q in enumerate(qs)]
            post(("m3", qs, w), ("m3", qs), values, dev(dy=s))

    def settle(qs):
        wait_for(("m2", qs), 2, len(qs))
        wait_for(("m3", qs), 2, len(qs))

    def here(qs, q, w):
        j = qs.index(q)
        return piece(0, q, w) + decode(("m2", qs, 1 - w), j) + decode(("m3", qs, w), j)

    def cross(i, w):
        post(("x", i, w), ("x", i, w), [piece(i, 0, w, 1)], dev(flip=True))

    def crossed(i, w):
        wait_for(("x", i, w), 1, 1)
        return piece(i, 1, w, 1) + decode(("x", i, w))

    def late_first():
        for w, _, s in ways:
            post(("n1", w), "n1", [crossed(2, w)], dev(dy=s))

    def late_second():
        for w, i, s in ways:
            post(("n2", w), "n2", [crossed(i, 1 - w)], dev(dy=s))

    def late_third():
        wait_for("n1", 2, 1)
        for w, i, s in ways:
            post(("n3", w), "n3", [crossed(i, w) + decode(("n1", w))], dev(dy=s))

    def store(w, late, total):
        gi_ref[pl.ds(late * 2 * PIECE + w * PIECE, PIECE), :] = total.astype(jnp.bfloat16)

    both, theirs, ours = (0, 1), (0,), (1,)

    multiply(2, 2)
    cross(2, 0)
    cross(2, 1)
    first(both)
    multiply(1, 1)
    second(both, ways[0])
    cross(1, 1)
    multiply(3, -1)
    cross(3, 0)
    second(both, ways[1])
    cross(1, 0)
    cross(3, 1)
    multiply(0, 0)
    cross(0, 0)
    cross(0, 1)
    third(both)
    late_first()
    late_second()

    arrived("iy20", rows_in(2, False, 0, zn))
    arrived("iy22", rows_in(2, True, 0, zn))
    arrived("jz", inall.at[pl.ds(0, 4 * yn)])

    def flip(i, _):
        rows = pl.ds(pl.multiple_of(i * BLOCK, BLOCK), BLOCK)
        for j in range(hid // BLOCK):
            cols = pl.ds(j * BLOCK, BLOCK)
            flipped[cols, rows] = inall[rows, cols].T
        return 0

    lax.fori_loop(0, TOKENS // BLOCK, flip, 0)

    def weight_grad(n, _):
        right = gall[:, pl.ds(pl.multiple_of(n * 256, 256), 256)]
        for i in range(hid // BLOCK):
            rows = pl.ds(i * BLOCK, BLOCK)
            product = jnp.dot(flipped[rows, :], right, preferred_element_type=jnp.float32)
            for j in range(2):
                m = mask[i, row * (wid // BLOCK) + n * 2 + j].astype(jnp.float32)
                gw_ref[rows, pl.ds(pl.multiple_of(n * 256 + j * BLOCK, BLOCK), BLOCK)] = (
                    product[:, j * BLOCK : (j + 1) * BLOCK] * m
                ).astype(jnp.bfloat16)
        return 0

    lax.fori_loop(0, wid // 256, weight_grad, 0)
    store_gw = pltpu.make_async_copy(gw_ref, gw_out, lsem.at[2])
    store_gw.start()

    settle(both)
    post("mz", "mz", [here(both, 0, w) for w in (0, 1)], dev(flip=True))
    late_third()
    wait_for("n2", 2, 1)
    wait_for("n3", 2, 1)
    for w in (0, 1):
        store(w, 1, crossed(0, w) + decode(("n2", 1 - w)) + decode(("n3", w)))
    wait_for("mz", 1, 2)
    for w in (0, 1):
        store(w, 0, here(both, 1, w) + decode("mz", w))
    store_gi = pltpu.make_async_copy(gi_ref, gi_out, lsem.at[0])
    store_gi.start()

    for kind, ref in kinds.items():
        sent = ref.at[pl.ds(0, leading[kind])]
        remote(kind, "c", sent, sent, dev(core=True)).wait_send()
    store_gw.wait()
    store_gi.wait()


def put(gi, gw, gi_out, gw_out, sem):
    n = gw.shape[0] // 7
    copies = [pltpu.make_async_copy(gi, gi_out, sem.at[7])]
    for i in range(7):
        rows = pl.ds(i * n, n)
        copies.append(pltpu.make_async_copy(gw.at[rows], gw_out.at[rows], sem.at[i]))
    for c in copies:
        c.start()
    for c in copies:
        c.wait()


def per_device(grad_output, inputs, weight, block_mask):
    hid, wid = weight.shape
    anywhere = pl.BlockSpec(memory_space=pl.ANY)
    near = pl.BlockSpec(memory_space=pltpu.VMEM)
    codes = [pltpu.VMEM((28, PIECE, hid), jnp.int16)] * 2
    scales = [pltpu.VMEM((24, 1, hid), jnp.float32)] * 2
    results = pl.pallas_call(
        kernel,
        out_shape=(pltpu.VMEM((ROWS, hid), jnp.bfloat16), pltpu.VMEM((hid, wid), jnp.bfloat16)),
        in_specs=[anywhere] * 4,
        out_specs=(anywhere, anywhere),
        scratch_shapes=[
            pltpu.SMEM(block_mask.shape, jnp.int32),
            pltpu.VMEM((ROWS, hid), jnp.bfloat16),
            pltpu.VMEM((hid, wid), jnp.bfloat16),
            pltpu.VMEM((TOKENS, wid), jnp.bfloat16),
            pltpu.VMEM((TOKENS, hid), jnp.bfloat16),
            pltpu.VMEM((hid, TOKENS), jnp.bfloat16),
            pltpu.VMEM((hid, wid), jnp.bfloat16),
            pltpu.VMEM((4, 256, hid), jnp.float32),
            *codes,
            *scales,
            pltpu.SemaphoreType.DMA((4,)),
            pltpu.SemaphoreType.DMA((60,)),
            pltpu.SemaphoreType.DMA((4,)),
        ],
        compiler_params=pltpu.CompilerParams(
            collective_id=0, has_side_effects=True, vmem_limit_bytes=56 << 20
        ),
        name="down_projection_backward",
    )(grad_output, inputs, weight, block_mask)
    return pl.pallas_call(
        put,
        out_shape=(
            jax.ShapeDtypeStruct((ROWS, hid), jnp.bfloat16),
            jax.ShapeDtypeStruct((hid, wid), jnp.bfloat16),
        ),
        in_specs=[near, near],
        out_specs=(anywhere, anywhere),
        scratch_shapes=[pltpu.SemaphoreType.DMA((8,))],
        name="put",
    )(*(pltpu.with_memory_space_constraint(r, pltpu.VMEM) for r in results))


def solution(mesh):
    return jax.shard_map(
        per_device,
        mesh=mesh,
        in_specs=(P("col", "row"), P("row", "col"), P("col", "row"), P("col", None)),
        out_specs=(P("row", "col"), P("col", "row")),
        check_vma=False,
    )
```

```python
import functools

import jax
import jax.numpy as jnp
from jax import lax
from jax.experimental import pallas as pl
from jax.experimental.pallas import tpu as pltpu
from jax.sharding import PartitionSpec as P

MESH = pl.DeviceIdType.MESH
BLOCK = 128
TOKENS = 1024
MINE = 32
ROWS = 128
ZFIRST = 64
PIECE = 32
TOP = 32767.0
RELAYED = (1, -1)


def wrap(v, n):
    return lax.rem(v + n, n)


def kernel(
    g_hbm, in_hbm, w_hbm, mask_hbm, gi_out, gw_out,
    mask, gi_ref, gw_ref, gall, inall, flipped, kept, part, grad,
    code_out, code_in, scale_out, scale_in,
    ssem, rsem, lsem,
):
    row, col = lax.axis_index("row"), lax.axis_index("col")
    y, zl = row // 2, lax.rem(row, 2)
    zh, x, k = col // 8, lax.rem(col // 2, 4), lax.rem(col, 2)
    hid, wid = w_hbm.shape

    def dev(dy=0, flip=False, dzh=0, dx=0, core=False):
        z = 1 - zl if flip else zl
        c = 1 - k if core else k
        return (wrap(y + dy, 4) * 2 + z, (wrap(zh + dzh, 4) * 4 + wrap(x + dx, 4)) * 2 + c)

    peers = [
        dev(dy=1), dev(dy=-1), dev(flip=True), dev(dzh=1), dev(dzh=-1),
        dev(dx=1), dev(dx=-1), dev(core=True),
    ]
    peers.append(dev(dx=2))

    load_g = pltpu.make_async_copy(
        g_hbm, gall.at[pl.ds(pl.multiple_of(col * MINE, MINE), MINE)], lsem.at[0]
    )
    load_in = pltpu.make_async_copy(
        in_hbm, inall.at[pl.ds(pl.multiple_of(row * ROWS, ROWS), ROWS)], lsem.at[1]
    )
    load_w = pltpu.make_async_copy(w_hbm, kept, lsem.at[2])
    load_mask = pltpu.make_async_copy(mask_hbm, mask, lsem.at[3])
    for load in (load_g, load_in, load_mask, load_w):
        load.start()

    barrier = pltpu.get_barrier_semaphore()
    for peer in peers:
        pl.semaphore_signal(barrier, inc=1, device_id=peer, device_id_type=MESH)
    pl.semaphore_wait(barrier, len(peers))
    load_g.wait()
    load_in.wait()

    kinds = {"g": gall, "in": inall, "code": code_out, "scale": scale_out}
    order = list(kinds)
    leading = dict.fromkeys(kinds, 0)
    names = {}

    def remote(kind, name, src, dst, device):
        i = names.setdefault(name, len(names))
        return pltpu.make_async_remote_copy(
            src_ref=src, dst_ref=dst, send_sem=ssem.at[order.index(kind)], recv_sem=rsem.at[i],
            device_id=device, device_id_type=MESH,
        )

    def send(kind, name, src, dst, device):
        leading[kind] += src.shape[0]
        remote(kind, name, src, dst, device).start()

    def arrived(name, ref):
        remote("g", name, ref, ref, dev(core=True)).wait_recv()

    def g(dz, dx, half=None):
        at = ((wrap(zh + dz, 4) * 4 + wrap(x + dx, 4)) * 2 + k) * MINE
        if half is None:
            return gall.at[pl.ds(pl.multiple_of(at, MINE), MINE)]
        n = MINE // 2
        return gall.at[pl.ds(pl.multiple_of(at + half * n, n), n)]

    def send_g(name, ref, device):
        send("g", name, ref, ref, device)

    def across(d, e):
        send_g("c", g(d, e), dev(core=True))

    def spread_z():
        for name, dz, part in (("zp", 1, 0), ("zm", -1, 1), ("zp", 1, 1), ("zm", -1, 0)):
            send_g((name, part), g(0, 0, part), dev(dzh=dz))

    def spread_x(d, part=None):
        send_g(("xp", d, part), g(d, 0, part), dev(dx=1))
        send_g(("xm", d, part), g(d, 0, part), dev(dx=-1))
        if d not in RELAYED:
            send_g(("x2", d), g(d, 0, part), dev(dx=2))
        send_g("c", g(d, 0, part), dev(core=True))

    def near_z():
        for name, d, part, on in (("zp", -1, 0, 1), ("zm", 1, 1, -1), ("zp", -1, 1, 0), ("zm", 1, 0, 0)):
            arrived((name, part), g(d, 0, part))
            if on:
                send_g("z2", g(d, 0, part), dev(dzh=on))
            spread_x(d, part)

    def near_x(d):
        halves = abs(d) == 1
        for name, e, part in (("xp", -1, 0), ("xm", 1, 1)):
            if halves:
                arrived((name, d, part), g(d, e, part))
            else:
                arrived((name, d, None), g(d, e))
            if d in RELAYED:
                send_g(("x2", d), g(d, e, part), dev(dx=-e))
        for name, e, part in (("xp", -1, 1), ("xm", 1, 0)):
            if halves:
                arrived((name, d, part), g(d, e, part))
            across(d, e)

    def finish_x(d):
        arrived(("x2", d), g(d, 2))
        across(d, 2)

    def rows_in(dy, flip, lo, n):
        z = 1 - zl if flip else zl
        at = (wrap(y + dy, 4) * 2 + z) * ROWS + lo
        return inall.at[pl.ds(pl.multiple_of(at, 8), n)]

    def send_in(name, dy, flip, lo, n, device):
        ref = rows_in(dy, flip, lo, n)
        send("in", name, ref, ref, device)

    def spread_y(tag, flip, lo, n):
        send_in("iyp" + tag, 0, flip, lo, n, dev(dy=1))
        send_in("iym" + tag, 0, flip, lo, n, dev(dy=-1))

    def relay_y(tag, flip, lo, n):
        h = n // 2
        arrived("iyp" + tag, rows_in(-1, flip, lo, n))
        send_in("iy2" + tag, -1, flip, lo, h, dev(dy=1))
        arrived("iym" + tag, rows_in(1, flip, lo, n))
        send_in("iy2" + tag, 1, flip, lo + h, h, dev(dy=-1))

    zn, yn = ZFIRST, ROWS - ZFIRST

    spread_z()
    spread_x(0)
    spread_y("1", False, zn, yn)
    spread_y("0", False, 0, zn)
    send_in("iza", 0, False, 0, zn // 2, dev(flip=True))

    load_mask.wait()
    load_w.wait()

    def mask_row(i, _):
        rows = pl.ds(pl.multiple_of(i * BLOCK, BLOCK), BLOCK)
        for j in range(wid // BLOCK):
            cols = pl.ds(j * BLOCK, BLOCK)
            m = mask[i, row * (wid // BLOCK) + j].astype(jnp.float32)
            kept[rows, cols] = (kept[rows, cols].astype(jnp.float32) * m).astype(jnp.bfloat16)
        return 0

    lax.fori_loop(0, hid // BLOCK, mask_row, 0)

    near_x(0)
    near_z()
    send_in("izb", 0, False, zn // 2, zn // 2, dev(flip=True))
    relay_y("1", False, zn, yn)
    finish_x(0)
    relay_y("0", False, 0, zn)
    arrived("iza", rows_in(0, True, 0, zn // 2))
    spread_y("2", True, 0, zn // 2)
    near_x(-1)
    arrived("z2", g(2, 0))
    spread_x(2)
    arrived("izb", rows_in(0, True, zn // 2, zn // 2))
    spread_y("3", True, zn // 2, zn // 2)
    send_in("jz", 0, False, zn, yn, dev(flip=True))
    send_in("jz", -1, False, zn, yn, dev(flip=True))
    send_in("jz", 1, False, zn, yn, dev(flip=True))
    near_x(1)
    arrived("iy21", rows_in(2, False, zn, yn))
    send_in("jz", 2, False, zn, yn, dev(flip=True))
    finish_x(-1)
    finish_x(1)
    near_x(2)
    relay_y("2", True, 0, zn // 2)
    relay_y("3", True, zn // 2, zn // 2)
    finish_x(2)
    arrived("c", gall.at[pl.ds(0, TOKENS // 2)])

    def multiply(i, dy):
        tokens = gall[pl.ds(pl.multiple_of(wrap(y + dy, 4) * 256, 256), 256), :]
        for lo in range(0, hid, 256):
            n = min(256, hid - lo)
            part[i, :, pl.ds(lo, n)] = lax.dot_general(
                tokens, kept[pl.ds(lo, n), :], (((1,), (1,)), ((), ())),
                preferred_element_type=jnp.float32,
            )

    def piece(i, q, w, late=0):
        z = zl if q else 1 - zl
        at = z * ROWS + late * 2 * PIECE + w * PIECE
        return part[i, pl.ds(pl.multiple_of(at, PIECE), PIECE), :]

    slots = {}
    used = [0, 0]

    def post(name, sem, values, device):
        c, m, n = slots[name] = (used[0], used[1], len(values))
        used[0] += n
        used[1] += 1
        top = functools.reduce(
            jnp.maximum, [jnp.max(jnp.abs(v), axis=0, keepdims=True) for v in values]
        )
        top = jnp.maximum(top, 1e-30)
        scale_out[m] = top * (1.0 / TOP)
        for j, v in enumerate(values):
            code_out[c + j] = jnp.round(v * (TOP / top)).astype(jnp.int32).astype(jnp.int16)
        cs, ms = pl.ds(c, n), pl.ds(m, 1)
        send("scale", (sem, "s"), scale_out.at[ms], scale_in.at[ms], device)
        send("code", (sem, "q"), code_out.at[cs], code_in.at[cs], device)

    def wait_for(sem, messages, n):
        arrived((sem, "s"), scale_in.at[pl.ds(0, messages)])
        arrived((sem, "q"), code_in.at[pl.ds(0, messages * n)])

    def decode(name, j=0):
        c, m, _ = slots[name]
        return code_in[c + j].astype(jnp.int32).astype(jnp.float32) * scale_in[m]

    ways = ((0, 1, 1), (1, 3, -1))

    def first(qs):
        for w, _, s in ways:
            post(("m1", qs, w), ("m1", qs), [piece(2, q, w) for q in qs], dev(dy=s))

    def second(qs, way):
        w, i, s = way
        post(("m2", qs, w), ("m2", qs), [piece(i, q, 1 - w) for q in qs], dev(dy=s))

    def third(qs):
        for w, i, s in ways:
            values = [piece(i, q, w) + decode(("m1", both, w), q) for q in qs]
            post(("m3", qs, w), ("m3", qs), values, dev(dy=s))

    def here(q, w):
        return piece(0, q, w) + decode(("m2", both, 1 - w), q) + decode(("m3", (q,), w))

    def cross(i, w):
        post(("x", i, w), ("x", i, w), [piece(i, 0, w, 1)], dev(flip=True))

    def crossed(i, w):
        wait_for(("x", i, w), 1, 1)
        return piece(i, 1, w, 1) + decode(("x", i, w))

    def late_first():
        for w, _, s in ways:
            post(("n1", w), "n1", [crossed(2, w)], dev(dy=s))

    def late_second():
        for w, i, s in ways:
            post(("n2", w), "n2", [crossed(i, 1 - w)], dev(dy=s))

    def late_third():
        wait_for("n1", 2, 1)
        for w, i, s in ways:
            post(("n3", w), "n3", [crossed(i, w) + decode(("n1", w))], dev(dy=s))

    def store(w, late, total):
        gi_ref[pl.ds(late * 2 * PIECE + w * PIECE, PIECE), :] = total.astype(jnp.bfloat16)

    def tokens(i, flip, lo, n):
        z = 1 - zl if flip else zl
        return pl.ds(pl.multiple_of((i * 2 + z) * ROWS + lo, 16), n)

    early = [tokens(i, False, 0, ROWS) for i in range(4)] + [tokens(i, True, 0, zn) for i in range(4)]
    late = [tokens(i, True, zn, yn) for i in range(4)]
    n_early = 4 * (ROWS + zn)

    def turn(groups, at):
        def turn_cols(j, _):
            cols = pl.ds(pl.multiple_of(j * BLOCK, BLOCK), BLOCK)
            for i, group in enumerate(groups):
                rows = jnp.concatenate([inall[t, cols] for t in group], axis=0)
                flipped[cols, pl.ds(at + i * BLOCK, BLOCK)] = rows.T
            return 0

        lax.fori_loop(0, hid // BLOCK, turn_cols, 0)

    def blocks(parts, n):
        c = BLOCK // n
        return [parts[i : i + c] for i in range(0, len(parts), c)]

    def early_grad(n, _):
        cols = pl.ds(pl.multiple_of(n * 256, 256), 256)
        right = jnp.concatenate([gall[t, cols] for t in early], axis=0)
        for i in range(0, hid, BLOCK):
            rows = pl.ds(i, BLOCK)
            grad[rows, cols] = jnp.dot(
                flipped[rows, pl.ds(0, n_early)], right, preferred_element_type=jnp.float32
            )
        return 0

    def late_grad(n, _):
        cols = pl.ds(pl.multiple_of(n * 256, 256), 256)
        right = jnp.concatenate([gall[t, cols] for t in late], axis=0)
        for i in range(hid // BLOCK):
            rows = pl.ds(i * BLOCK, BLOCK)
            product = grad[rows, cols] + jnp.dot(
                flipped[rows, pl.ds(n_early, 4 * yn)], right, preferred_element_type=jnp.float32
            )
            for j in range(2):
                m = mask[i, row * (wid // BLOCK) + n * 2 + j].astype(jnp.float32)
                gw_ref[rows, pl.ds(pl.multiple_of(n * 256 + j * BLOCK, BLOCK), BLOCK)] = (
                    product[:, j * BLOCK : (j + 1) * BLOCK] * m
                ).astype(jnp.bfloat16)
        return 0

    both, theirs, ours = (0, 1), (0,), (1,)

    multiply(2, 2)
    cross(2, 0)
    cross(2, 1)
    first(both)
    multiply(1, 1)
    second(both, ways[0])
    cross(1, 1)
    multiply(3, -1)
    cross(3, 0)
    second(both, ways[1])
    cross(1, 0)
    cross(3, 1)
    multiply(0, 0)
    cross(0, 0)
    cross(0, 1)
    arrived("iy20", rows_in(2, False, 0, zn))
    arrived("iy22", rows_in(2, True, 0, zn // 2))
    arrived("iy23", rows_in(2, True, zn // 2, zn // 2))
    turn([[t] for t in early[:4]] + blocks(early[4:], zn), 0)
    lax.fori_loop(0, 2, early_grad, 0)
    wait_for(("m1", both), 2, 2)
    third(theirs)
    late_first()
    third(ours)
    late_second()
    lax.fori_loop(2, wid // 256, early_grad, 0)

    wait_for(("m2", both), 2, 2)
    wait_for(("m3", theirs), 2, 1)
    post("mz", "mz", [here(0, w) for w in (0, 1)], dev(flip=True))
    late_third()

    arrived("jz", inall.at[pl.ds(0, 4 * yn)])
    turn(blocks(late, yn), n_early)
    lax.fori_loop(0, wid // 256, late_grad, 0)
    store_gw = pltpu.make_async_copy(gw_ref, gw_out, lsem.at[2])
    store_gw.start()

    wait_for("n2", 2, 1)
    wait_for("n3", 2, 1)
    for w in (0, 1):
        store(w, 1, crossed(0, w) + decode(("n2", 1 - w)) + decode(("n3", w)))
    wait_for(("m3", ours), 2, 1)
    wait_for("mz", 1, 2)
    for w in (0, 1):
        store(w, 0, here(1, w) + decode("mz", w))
    store_gi = pltpu.make_async_copy(gi_ref, gi_out, lsem.at[0])
    store_gi.start()

    for kind, ref in kinds.items():
        sent = ref.at[pl.ds(0, leading[kind])]
        remote(kind, "c", sent, sent, dev(core=True)).wait_send()
    store_gw.wait()
    store_gi.wait()


def put(gi, gw, gi_out, gw_out, sem):
    n = gw.shape[0] // 7
    copies = [pltpu.make_async_copy(gi, gi_out, sem.at[7])]
    for i in range(7):
        rows = pl.ds(i * n, n)
        copies.append(pltpu.make_async_copy(gw.at[rows], gw_out.at[rows], sem.at[i]))
    for c in copies:
        c.start()
    for c in copies:
        c.wait()


def per_device(grad_output, inputs, weight, block_mask):
    hid, wid = weight.shape
    anywhere = pl.BlockSpec(memory_space=pl.ANY)
    near = pl.BlockSpec(memory_space=pltpu.VMEM)
    codes = [pltpu.VMEM((28, PIECE, hid), jnp.int16)] * 2
    scales = [pltpu.VMEM((28, 1, hid), jnp.float32)] * 2
    results = pl.pallas_call(
        kernel,
        out_shape=(pltpu.VMEM((ROWS, hid), jnp.bfloat16), pltpu.VMEM((hid, wid), jnp.bfloat16)),
        in_specs=[anywhere] * 4,
        out_specs=(anywhere, anywhere),
        scratch_shapes=[
            pltpu.SMEM(block_mask.shape, jnp.int32),
            pltpu.VMEM((ROWS, hid), jnp.bfloat16),
            pltpu.VMEM((hid, wid), jnp.bfloat16),
            pltpu.VMEM((TOKENS, wid), jnp.bfloat16),
            pltpu.VMEM((TOKENS, hid), jnp.bfloat16),
            pltpu.VMEM((hid, TOKENS), jnp.bfloat16),
            pltpu.VMEM((hid, wid), jnp.bfloat16),
            pltpu.VMEM((4, 256, hid), jnp.float32),
            pltpu.VMEM((hid, wid), jnp.float32),
            *codes,
            *scales,
            pltpu.SemaphoreType.DMA((4,)),
            pltpu.SemaphoreType.DMA((80,)),
            pltpu.SemaphoreType.DMA((4,)),
        ],
        compiler_params=pltpu.CompilerParams(
            collective_id=0, has_side_effects=True, vmem_limit_bytes=56 << 20
        ),
        name="down_projection_backward",
    )(grad_output, inputs, weight, block_mask)
    return pl.pallas_call(
        put,
        out_shape=(
            jax.ShapeDtypeStruct((ROWS, hid), jnp.bfloat16),
            jax.ShapeDtypeStruct((hid, wid), jnp.bfloat16),
        ),
        in_specs=[near, near],
        out_specs=(anywhere, anywhere),
        scratch_shapes=[pltpu.SemaphoreType.DMA((8,))],
        name="put",
    )(*(pltpu.with_memory_space_constraint(r, pltpu.VMEM) for r in results))


def solution(mesh):
    return jax.shard_map(
        per_device,
        mesh=mesh,
        in_specs=(P("col", "row"), P("row", "col"), P("col", "row"), P("col", None)),
        out_specs=(P("row", "col"), P("col", "row")),
        check_vma=False,
    )
```

```python
import functools

import jax
import jax.numpy as jnp
from jax import lax
from jax.experimental import pallas as pl
from jax.experimental.pallas import tpu as pltpu
from jax.sharding import PartitionSpec as P

MESH = pl.DeviceIdType.MESH
BLOCK = 128
TOKENS = 1024
MINE = 32
ROWS = 128
ZFIRST = 64
PIECE = 32
TOP = 32767.0
RELAYED = (1, -1)


def wrap(v, n):
    return lax.rem(v + n, n)


def kernel(
    g_hbm, in_hbm, w_hbm, mask_hbm, gi_out, gw_out,
    mask, gi_ref, gw_ref, gall, inall, flipped, kept, part, grad,
    code_out, code_in, scale_out, scale_in,
    ssem, rsem, lsem,
):
    row, col = lax.axis_index("row"), lax.axis_index("col")
    y, zl = row // 2, lax.rem(row, 2)
    zh, x, k = col // 8, lax.rem(col // 2, 4), lax.rem(col, 2)
    hid, wid = w_hbm.shape

    def dev(dy=0, flip=False, dzh=0, dx=0, core=False):
        z = 1 - zl if flip else zl
        c = 1 - k if core else k
        return (wrap(y + dy, 4) * 2 + z, (wrap(zh + dzh, 4) * 4 + wrap(x + dx, 4)) * 2 + c)

    peers = [
        dev(dy=1), dev(dy=-1), dev(flip=True), dev(dzh=1), dev(dzh=-1),
        dev(dx=1), dev(dx=-1), dev(core=True),
    ]
    peers.append(dev(dx=2))

    load_g = pltpu.make_async_copy(
        g_hbm, gall.at[pl.ds(pl.multiple_of(col * MINE, MINE), MINE)], lsem.at[0]
    )
    load_in = pltpu.make_async_copy(
        in_hbm, inall.at[pl.ds(pl.multiple_of(row * ROWS, ROWS), ROWS)], lsem.at[1]
    )
    load_w = pltpu.make_async_copy(w_hbm, kept, lsem.at[2])
    load_mask = pltpu.make_async_copy(mask_hbm, mask, lsem.at[3])
    for load in (load_g, load_in, load_mask, load_w):
        load.start()

    barrier = pltpu.get_barrier_semaphore()
    for peer in peers:
        pl.semaphore_signal(barrier, inc=1, device_id=peer, device_id_type=MESH)
    pl.semaphore_wait(barrier, len(peers))
    load_g.wait()
    load_in.wait()

    kinds = {"g": gall, "in": inall, "code": code_out, "scale": scale_out}
    order = list(kinds)
    leading = dict.fromkeys(kinds, 0)
    names = {}

    def remote(kind, name, src, dst, device):
        i = names.setdefault(name, len(names))
        return pltpu.make_async_remote_copy(
            src_ref=src, dst_ref=dst, send_sem=ssem.at[order.index(kind)], recv_sem=rsem.at[i],
            device_id=device, device_id_type=MESH,
        )

    def send(kind, name, src, dst, device):
        leading[kind] += src.shape[0]
        remote(kind, name, src, dst, device).start()

    def arrived(name, ref):
        remote("g", name, ref, ref, dev(core=True)).wait_recv()

    def g(dz, dx, half=None):
        at = ((wrap(zh + dz, 4) * 4 + wrap(x + dx, 4)) * 2 + k) * MINE
        if half is None:
            return gall.at[pl.ds(pl.multiple_of(at, MINE), MINE)]
        n = MINE // 2
        return gall.at[pl.ds(pl.multiple_of(at + half * n, n), n)]

    def send_g(name, ref, device):
        send("g", name, ref, ref, device)

    def across(d, e):
        send_g("c", g(d, e), dev(core=True))

    def spread_z():
        for name, dz, part in (("zp", 1, 0), ("zm", -1, 1), ("zp", 1, 1), ("zm", -1, 0)):
            send_g((name, part), g(0, 0, part), dev(dzh=dz))

    def spread_x(d, part=None):
        send_g(("xp", d, part), g(d, 0, part), dev(dx=1))
        send_g(("xm", d, part), g(d, 0, part), dev(dx=-1))
        if d not in RELAYED:
            send_g(("x2", d), g(d, 0, part), dev(dx=2))
        send_g("c", g(d, 0, part), dev(core=True))

    def near_z():
        for name, d, part, on in (("zp", -1, 0, 1), ("zm", 1, 1, -1), ("zp", -1, 1, 0), ("zm", 1, 0, 0)):
            arrived((name, part), g(d, 0, part))
            if on:
                send_g("z2", g(d, 0, part), dev(dzh=on))
            spread_x(d, part)

    def near_x(d):
        halves = abs(d) == 1
        for name, e, part in (("xp", -1, 0), ("xm", 1, 1)):
            if halves:
                arrived((name, d, part), g(d, e, part))
            else:
                arrived((name, d, None), g(d, e))
            if d in RELAYED:
                send_g(("x2", d), g(d, e, part), dev(dx=-e))
        for name, e, part in (("xp", -1, 1), ("xm", 1, 0)):
            if halves:
                arrived((name, d, part), g(d, e, part))
            across(d, e)

    def finish_x(d):
        arrived(("x2", d), g(d, 2))
        across(d, 2)

    def rows_in(dy, flip, lo, n):
        z = 1 - zl if flip else zl
        at = (wrap(y + dy, 4) * 2 + z) * ROWS + lo
        return inall.at[pl.ds(pl.multiple_of(at, 8), n)]

    def send_in(name, dy, flip, lo, n, device):
        ref = rows_in(dy, flip, lo, n)
        send("in", name, ref, ref, device)

    def spread_y(tag, flip, lo, n):
        send_in("iyp" + tag, 0, flip, lo, n, dev(dy=1))
        send_in("iym" + tag, 0, flip, lo, n, dev(dy=-1))

    def relay_y(tag, flip, lo, n):
        h = n // 2
        arrived("iyp" + tag, rows_in(-1, flip, lo, n))
        send_in("iy2" + tag, -1, flip, lo, h, dev(dy=1))
        arrived("iym" + tag, rows_in(1, flip, lo, n))
        send_in("iy2" + tag, 1, flip, lo + h, h, dev(dy=-1))

    zn, yn = ZFIRST, ROWS - ZFIRST

    spread_z()
    spread_x(0)
    spread_y("1", False, zn, yn)
    spread_y("0", False, 0, zn)

    load_mask.wait()
    load_w.wait()

    def mask_row(i, _):
        rows = pl.ds(pl.multiple_of(i * BLOCK, BLOCK), BLOCK)
        for j in range(wid // BLOCK):
            cols = pl.ds(j * BLOCK, BLOCK)
            m = mask[i, row * (wid // BLOCK) + j].astype(jnp.float32)
            kept[rows, cols] = (kept[rows, cols].astype(jnp.float32) * m).astype(jnp.bfloat16)
        return 0

    lax.fori_loop(0, hid // BLOCK, mask_row, 0)

    near_x(0)
    near_z()
    send_in("iza", 0, False, 0, zn // 2, dev(flip=True))
    send_in("izb", 0, False, zn // 2, zn // 2, dev(flip=True))
    relay_y("1", False, zn, yn)
    finish_x(0)
    relay_y("0", False, 0, zn)
    arrived("iza", rows_in(0, True, 0, zn // 2))
    spread_y("2", True, 0, zn // 2)
    near_x(-1)
    near_x(1)
    arrived("z2", g(2, 0))
    spread_x(2)
    arrived("izb", rows_in(0, True, zn // 2, zn // 2))
    spread_y("3", True, zn // 2, zn // 2)
    send_in("jz", 0, False, zn, yn, dev(flip=True))
    send_in("jz", -1, False, zn, yn, dev(flip=True))
    send_in("jz", 1, False, zn, yn, dev(flip=True))
    arrived("iy21", rows_in(2, False, zn, yn))
    send_in("jz", 2, False, zn, yn, dev(flip=True))
    finish_x(-1)
    finish_x(1)
    near_x(2)
    relay_y("2", True, 0, zn // 2)
    relay_y("3", True, zn // 2, zn // 2)
    finish_x(2)
    arrived("c", gall.at[pl.ds(0, TOKENS // 2)])

    def multiply(i, dy):
        tokens = gall[pl.ds(pl.multiple_of(wrap(y + dy, 4) * 256, 256), 256), :]
        for lo in range(0, hid, 256):
            n = min(256, hid - lo)
            part[i, :, pl.ds(lo, n)] = lax.dot_general(
                tokens, kept[pl.ds(lo, n), :], (((1,), (1,)), ((), ())),
                preferred_element_type=jnp.float32,
            )

    def piece(i, q, w, late=0):
        z = zl if q else 1 - zl
        at = z * ROWS + late * 2 * PIECE + w * PIECE
        return part[i, pl.ds(pl.multiple_of(at, PIECE), PIECE), :]

    slots = {}
    used = [0, 0]

    def post(name, sem, values, device):
        c, m, n = slots[name] = (used[0], used[1], len(values))
        used[0] += n
        used[1] += 1
        top = functools.reduce(
            jnp.maximum, [jnp.max(jnp.abs(v), axis=0, keepdims=True) for v in values]
        )
        top = jnp.maximum(top, 1e-30)
        scale_out[m] = top * (1.0 / TOP)
        for j, v in enumerate(values):
            code_out[c + j] = jnp.round(v * (TOP / top)).astype(jnp.int32).astype(jnp.int16)
        cs, ms = pl.ds(c, n), pl.ds(m, 1)
        send("scale", sem, scale_out.at[ms], scale_in.at[ms], device)
        send("code", sem, code_out.at[cs], code_in.at[cs], device)

    def wait_for(sem, messages, n):
        arrived(sem, scale_in.at[pl.ds(0, messages * (n * PIECE // 2 + 1))])

    def decode(name, j=0):
        c, m, _ = slots[name]
        return code_in[c + j].astype(jnp.int32).astype(jnp.float32) * scale_in[m]

    ways = ((0, 1, 1), (1, 3, -1))

    def first(qs):
        for w, _, s in ways:
            post(("m1", qs, w), ("m1", qs), [piece(2, q, w) for q in qs], dev(dy=s))

    def second(qs, way):
        w, i, s = way
        post(("m2", qs, w), ("m2", qs), [piece(i, q, 1 - w) for q in qs], dev(dy=s))

    def third(qs):
        for w, i, s in ways:
            values = [piece(i, q, w) + decode(("m1", both, w), q) for q in qs]
            post(("m3", qs, w), ("m3", qs), values, dev(dy=s))

    def here(q, w):
        return piece(0, q, w) + decode(("m2", both, 1 - w), q) + decode(("m3", (q,), w))

    def cross(i, w):
        post(("x", i, w), ("x", i, w), [piece(i, 0, w, 1)], dev(flip=True))

    def crossed(i, w):
        wait_for(("x", i, w), 1, 1)
        return piece(i, 1, w, 1) + decode(("x", i, w))

    def late_first():
        for w, _, s in ways:
            post(("n1", w), "n1", [crossed(2, w)], dev(dy=s))

    def late_second():
        for w, i, s in ways:
            post(("n2", w), "n2", [crossed(i, 1 - w)], dev(dy=s))

    def late_third():
        wait_for("n1", 2, 1)
        for w, i, s in ways:
            post(("n3", w), "n3", [crossed(i, w) + decode(("n1", w))], dev(dy=s))

    def store(w, late, total):
        gi_ref[pl.ds(late * 2 * PIECE + w * PIECE, PIECE), :] = total.astype(jnp.bfloat16)

    def tokens(i, flip, lo, n):
        z = 1 - zl if flip else zl
        return pl.ds(pl.multiple_of((i * 2 + z) * ROWS + lo, 16), n)

    step = 32
    early = [tokens(i, False, lo, step) for i in range(4) for lo in range(0, ROWS, step)]
    early += [tokens(i, True, lo, step) for i in range(4) for lo in range(0, zn, step)]
    late = [tokens(i, True, lo, step) for i in range(4) for lo in range(zn, ROWS, step)]
    n_early = 4 * (ROWS + zn)

    def turn(groups, at):
        def turn_cols(j, _):
            cols = pl.ds(pl.multiple_of(j * BLOCK, BLOCK), BLOCK)
            for i, group in enumerate(groups):
                rows = jnp.concatenate([inall[t, cols] for t in group], axis=0)
                flipped[cols, pl.ds(at + i * BLOCK, BLOCK)] = rows.T
            return 0

        lax.fori_loop(0, hid // BLOCK, turn_cols, 0)

    def blocks(parts):
        c = BLOCK // step
        return [parts[i : i + c] for i in range(0, len(parts), c)]

    def early_grad(n, _):
        cols = pl.ds(pl.multiple_of(n * 256, 256), 256)
        right = jnp.concatenate([gall[t, cols] for t in early], axis=0)
        for i in range(0, hid, BLOCK):
            rows = pl.ds(i, BLOCK)
            grad[rows, cols] = jnp.dot(
                flipped[rows, pl.ds(0, n_early)], right, preferred_element_type=jnp.float32
            )
        return 0

    def late_grad(n, _):
        cols = pl.ds(pl.multiple_of(n * 256, 256), 256)
        right = jnp.concatenate([gall[t, cols] for t in late], axis=0)
        for i in range(hid // BLOCK):
            rows = pl.ds(i * BLOCK, BLOCK)
            product = grad[rows, cols] + jnp.dot(
                flipped[rows, pl.ds(n_early, 4 * yn)], right, preferred_element_type=jnp.float32
            )
            for j in range(2):
                m = mask[i, row * (wid // BLOCK) + n * 2 + j].astype(jnp.float32)
                gw_ref[rows, pl.ds(pl.multiple_of(n * 256 + j * BLOCK, BLOCK), BLOCK)] = (
                    product[:, j * BLOCK : (j + 1) * BLOCK] * m
                ).astype(jnp.bfloat16)
        return 0

    both, theirs, ours = (0, 1), (0,), (1,)

    multiply(2, 2)
    cross(2, 0)
    cross(2, 1)
    first(both)
    multiply(1, 1)
    second(both, ways[0])
    cross(1, 1)
    multiply(3, -1)
    cross(3, 0)
    second(both, ways[1])
    cross(1, 0)
    cross(3, 1)
    multiply(0, 0)
    cross(0, 0)
    cross(0, 1)
    arrived("iy20", rows_in(2, False, 0, zn))
    arrived("iy22", rows_in(2, True, 0, zn // 2))
    arrived("iy23", rows_in(2, True, zn // 2, zn // 2))
    turn(blocks(early), 0)
    lax.fori_loop(0, 2, early_grad, 0)
    wait_for(("m1", both), 2, 2)
    third(theirs)
    late_first()
    third(ours)
    late_second()
    lax.fori_loop(2, wid // 256, early_grad, 0)

    wait_for(("m2", both), 2, 2)
    wait_for(("m3", theirs), 2, 1)
    post("mz", "mz", [here(0, w) for w in (0, 1)], dev(flip=True))
    late_third()

    arrived("jz", inall.at[pl.ds(0, 4 * yn)])
    turn(blocks(late), n_early)
    lax.fori_loop(0, wid // 256, late_grad, 0)
    store_gw = pltpu.make_async_copy(gw_ref, gw_out, lsem.at[2])
    store_gw.start()

    wait_for("n2", 2, 1)
    wait_for("n3", 2, 1)
    for w in (0, 1):
        store(w, 1, crossed(0, w) + decode(("n2", 1 - w)) + decode(("n3", w)))
    wait_for(("m3", ours), 2, 1)
    wait_for("mz", 1, 2)
    for w in (0, 1):
        store(w, 0, here(1, w) + decode("mz", w))
    store_gi = pltpu.make_async_copy(gi_ref, gi_out, lsem.at[0])
    store_gi.start()

    for kind, ref in kinds.items():
        sent = ref.at[pl.ds(0, leading[kind])]
        remote(kind, "c", sent, sent, dev(core=True)).wait_send()
    store_gw.wait()
    store_gi.wait()


def put(gi, gw, gi_out, gw_out, sem):
    copies = [
        pltpu.make_async_copy(gw, gw_out, sem.at[0]),
        pltpu.make_async_copy(gi, gi_out, sem.at[1]),
    ]
    for c in copies:
        c.start()
    for c in copies:
        c.wait()


def per_device(grad_output, inputs, weight, block_mask):
    hid, wid = weight.shape
    anywhere = pl.BlockSpec(memory_space=pl.ANY)
    near = pl.BlockSpec(memory_space=pltpu.VMEM)
    codes = [pltpu.VMEM((28, PIECE, hid), jnp.int16)] * 2
    scales = [pltpu.VMEM((n, 1, hid), jnp.float32) for n in (23, 66)]
    results = pl.pallas_call(
        kernel,
        out_shape=(pltpu.VMEM((ROWS, hid), jnp.bfloat16), pltpu.VMEM((hid, wid), jnp.bfloat16)),
        in_specs=[anywhere] * 4,
        out_specs=(anywhere, anywhere),
        scratch_shapes=[
            pltpu.SMEM(block_mask.shape, jnp.int32),
            pltpu.VMEM((ROWS, hid), jnp.bfloat16),
            pltpu.VMEM((hid, wid), jnp.bfloat16),
            pltpu.VMEM((TOKENS, wid), jnp.bfloat16),
            pltpu.VMEM((TOKENS, hid), jnp.bfloat16),
            pltpu.VMEM((hid, TOKENS), jnp.bfloat16),
            pltpu.VMEM((hid, wid), jnp.bfloat16),
            pltpu.VMEM((4, 256, hid), jnp.float32),
            pltpu.VMEM((hid, wid), jnp.float32),
            *codes,
            *scales,
            pltpu.SemaphoreType.DMA((4,)),
            pltpu.SemaphoreType.DMA((53,)),
            pltpu.SemaphoreType.DMA((4,)),
        ],
        compiler_params=pltpu.CompilerParams(
            collective_id=0, has_side_effects=True, vmem_limit_bytes=56 << 20
        ),
        name="down_projection_backward",
    )(grad_output, inputs, weight, block_mask)
    return pl.pallas_call(
        put,
        out_shape=(
            jax.ShapeDtypeStruct((ROWS, hid), jnp.bfloat16),
            jax.ShapeDtypeStruct((hid, wid), jnp.bfloat16),
        ),
        in_specs=[near, near],
        out_specs=(anywhere, anywhere),
        scratch_shapes=[pltpu.SemaphoreType.DMA((2,))],
        name="put",
    )(*(pltpu.with_memory_space_constraint(r, pltpu.VMEM) for r in results))


def solution(mesh):
    return jax.shard_map(
        per_device,
        mesh=mesh,
        in_specs=(P("col", "row"), P("row", "col"), P("col", "row"), P("col", None)),
        out_specs=(P("row", "col"), P("col", "row")),
        check_vma=False,
    )
```
